32 devices in a mesh: fsdp: 16 (over z, x, core), col: 2 (over y).
Axes of the slice: x: 2, y: 2, z: 4, core: 2. Of those that a mesh axis runs over, the one named last changes fastest.
Arguments:
- block_input: bfloat16 [2, 16, 128, 2048], P(None, 'fsdp', 'col'), may hold values from -6 to 6
- doc_lengths: int32 [2, 16, 4], P(None, 'fsdp'), may hold values from 1 to 96, 128 in all within a row
- norm_attn: bfloat16 [2048], P('fsdp'), may hold values from 0.099609375 to 1.8984375
- w_query: bfloat16 [2048, 2048], P('fsdp', 'col'), may hold values from -0.125 to 0.125
- w_key: bfloat16 [2048, 1024], P('fsdp', 'col'), may hold values from -0.125 to 0.125
- w_value: bfloat16 [2048, 1024], P('fsdp', 'col'), may hold values from -0.125 to 0.125
- w_gate_attn: bfloat16 [2048, 2048], P('fsdp', 'col'), may hold values from -0.125 to 0.125
- w_out: bfloat16 [2048, 2048], P('fsdp', 'col'), may hold values from -1 to 1
- gain_query: bfloat16 [128], P('fsdp'), may hold values from 0.099609375 to 1.8984375
- gain_key: bfloat16 [128], P('fsdp'), may hold values from 0.099609375 to 1.8984375
- norm_ffn: bfloat16 [2048], P('fsdp'), may hold values from 0.099609375 to 1.8984375
- w_gate: bfloat16 [2048, 6144], P('fsdp', 'col'), may hold values from -0.125 to 0.125
- w_up: bfloat16 [2048, 6144], P('fsdp', 'col'), may hold values from -0.125 to 0.125
- w_down: bfloat16 [6144, 2048], P('fsdp', 'col'), may hold values from -0.078125 to 0.078125
- grad_output: bfloat16 [2, 16, 128, 2048], P(None, 'fsdp', 'col'), may hold values from -6 to 6
Outputs:
- block_output: bfloat16 [2, 16, 128, 2048], P(None, 'fsdp', 'col')
- grad_input: float32 [2, 16, 128, 2048], P(None, 'fsdp', 'col')
- grad_norm_attn: float32 [2048], P('fsdp')
- grad_query: float32 [2048, 2048], P('fsdp', 'col')
- grad_key: float32 [2048, 1024], P('fsdp', 'col')
- grad_value: float32 [2048, 1024], P('fsdp', 'col')
- grad_gate_attn: float32 [2048, 2048], P('fsdp', 'col')
- grad_out: float32 [2048, 2048], P('fsdp', 'col')
- grad_gain_query: float32 [128], P('fsdp')
- grad_gain_key: float32 [128], P('fsdp')
- grad_norm_ffn: float32 [2048], P('fsdp')
- grad_gate: float32 [2048, 6144], P('fsdp', 'col')
- grad_up: float32 [2048, 6144], P('fsdp', 'col')
- grad_down: float32 [6144, 2048], P('fsdp', 'col')
The draws below stay inside these ranges and needn't reach their ends.
Inputs may be any that keep to these rules, and one draw needn't show every extreme that they name: `doc_lengths`: each bucket holds 4 documents packed in order from position 0; their lengths sum to 128, and in every bucket the longest has exactly 96 tokens.
All inputs are finite; a program needn't handle non-finite values.
Results may differ from the reference program's by a relative error of at most 0.014.
Values may be sent and summed in bfloat16 or wider, within the bound.
No kernel may reach another device: no remote copies, remote signals or barrier semaphores. Data moves between devices by JAX's collectives and lax.ppermute only.
A program may use at most 448 MiB of HBM per device.

```python
import math
import jax
import jax.numpy as jnp
import numpy as np
from jax import lax

D = 2048
H = 16
KVH = 8
HD = 128
FF = 6144
MB = 2
BUCKET = 128
NDOC = 4
MOST = 96
NSEQ = 16


def strengthened(result, own_key, source, target, blocks, factor):
    owner, partner = [(jnp.arange(result.shape[axis_at]) // (result.shape[axis_at] // blocks)).reshape([-1 if axis == axis_at else 1 for axis in range(result.ndim)]) for axis_at in (source, target)]
    chosen = jax.random.permutation(own_key, blocks)[partner]
    strong = (owner == chosen) | (owner == (partner + blocks // 2) % blocks)
    return jnp.where(strong, factor * result, result)


def levels(key, shape, split, smallest, high):
    def one(position, blocks):
        steps = jax.random.uniform(jax.random.fold_in(jax.random.fold_in(key, 6), position), (blocks,), jnp.float32, smallest / len(split), high / len(split))
        return jnp.repeat(jnp.exp(steps), shape[position] // blocks).reshape((-1,) + (1,) * (len(shape) - position - 1))

    gain = one(*split[0])
    for cut in split[1:]:
        gain = gain * one(*cut)
    return gain


def profile(count, total, reach, skew):
    loads = [(1 << 20) // math.isqrt(rank ** skew) + 1 for rank in range(2, count + 1)]
    spare, holding = total - reach - (count - 1), [1] * (count - 1)
    while spare > 0:
        free = [i for i in range(count - 1) if holding[i] < reach]
        whole, left = sum([loads[i] for i in free]), spare
        for i in free:
            addition = min(reach - holding[i], max(1, left * loads[i] // whole), spare)
            holding[i] = holding[i] + addition
            spare = spare - addition
    return np.array([reach] + holding)


def ragged_sizes(rng, amount, total, bound, slope):
    if amount == 2:
        one = jax.random.randint(rng, (), max(1, total - bound), min(bound, total - 1) + 1)
        return jnp.stack([one, total - one])
    tallies = jnp.asarray(profile(amount, total, bound, slope), jnp.int32)
    couples = (amount - 1) // 2
    donor, taker = tallies[1:1 + 2 * couples:2], tallies[2:2 + 2 * couples:2]
    room = jnp.minimum(donor - 1, bound - taker)
    moved = jax.random.randint(jax.random.fold_in(rng, 1), (couples,), 0, 1 << 20) % (room + 1)
    tallies = tallies.at[1:1 + 2 * couples:2].set(donor - moved).at[2:2 + 2 * couples:2].set(taker + moved)
    return tallies[jax.random.permutation(jax.random.fold_in(rng, 2), amount)]


def scatter_about(key, shape, width, most, pieces=(), held_as=jnp.bfloat16):
    drawn = width * jax.random.normal(key, shape, jnp.float32)
    if pieces:
        drawn = drawn * levels(key, shape, pieces, -0.22, 0.18)
    return jnp.clip(drawn, -most, most).astype(held_as)


def heavy_noise(stream_key, shape, scale, bound, cuts, heavy, held_as=jnp.bfloat16):
    result = scale * jax.random.normal(stream_key, shape, jnp.float32)
    if cuts:
        result = result * levels(stream_key, shape, cuts, -0.22, 0.18)
    return jnp.clip(strengthened(result, jax.random.fold_in(stream_key, 3), *heavy), -bound, bound).astype(held_as)


def setup_inputs(seed: int = 0) -> dict:
    key_of = jax.random.split(jax.random.key(seed), 16)
    block_input = heavy_noise(key_of[0], (MB, NSEQ, BUCKET, D), 1.0, 6.0, ((1, 16), (2, 2)), (1, 3, 16, 2.0))
    doc_lengths = jax.vmap(lambda own: ragged_sizes(own, NDOC, BUCKET, MOST, 2))(jax.random.split(key_of[1], MB * NSEQ)).reshape((MB, NSEQ, NDOC)).astype(jnp.int32)
    norm_attn = jnp.clip(1.0 + 0.18 * jax.random.normal(key_of[2], (D,), jnp.float32), 0.099609375, 1.8984375).astype(jnp.bfloat16)
    w_query = scatter_about(key_of[3], (D, H * HD), D ** -0.5, 0.125, ((0, 16), (1, 2)))
    w_key = scatter_about(key_of[4], (D, KVH * HD), D ** -0.5, 0.125, ((0, 16), (1, 2)))
    w_value = scatter_about(key_of[5], (D, KVH * HD), D ** -0.5, 0.125, ((0, 16), (1, 2)))
    w_gate_attn = scatter_about(key_of[6], (D, H * HD), D ** -0.5, 0.125, ((0, 16), (1, 2)))
    w_out = scatter_about(key_of[7], (H * HD, D), (H * HD // 64) ** -0.5, 1.0, ((0, 16), (1, 2)))
    gain_query = jnp.clip(1.0 + 0.18 * jax.random.normal(key_of[8], (HD,), jnp.float32), 0.099609375, 1.8984375).astype(jnp.bfloat16)
    gain_key = jnp.clip(1.0 + 0.18 * jax.random.normal(key_of[9], (HD,), jnp.float32), 0.099609375, 1.8984375).astype(jnp.bfloat16)
    norm_ffn = jnp.clip(1.0 + 0.18 * jax.random.normal(key_of[10], (D,), jnp.float32), 0.099609375, 1.8984375).astype(jnp.bfloat16)
    w_gate = scatter_about(key_of[11], (D, FF), D ** -0.5, 0.125, ((0, 16), (1, 2)))
    w_up = scatter_about(key_of[12], (D, FF), D ** -0.5, 0.125, ((0, 16), (1, 2)))
    w_down = scatter_about(key_of[13], (FF, D), FF ** -0.5, 0.078125, ((0, 16), (1, 2)))
    grad_output = heavy_noise(key_of[14], (MB, NSEQ, BUCKET, D), 1.0, 6.0, ((1, 16), (2, 2)), (1, 3, 16, 2.0))
    return {"block_input": block_input, "doc_lengths": doc_lengths, "norm_attn": norm_attn, "w_query": w_query, "w_key": w_key, "w_value": w_value, "w_gate_attn": w_gate_attn, "w_out": w_out, "gain_query": gain_query, "gain_key": gain_key, "norm_ffn": norm_ffn, "w_gate": w_gate, "w_up": w_up, "w_down": w_down, "grad_output": grad_output}


eps_norm = 1e-06
theta_base = 1000000.0
masked_score = -1e+30

@jax.custom_vjp
def low(v):
    return lax.optimization_barrier(v.astype(jnp.bfloat16)).astype(jnp.float32)

@jax.custom_vjp
def low_back(v):
    return v

def low_keep(v):
    return (low(v), None)

def low_pass(kept, grad):
    return (grad,)

def back_keep(v):
    return (v, None)

def back_low(kept, grad):
    return (low(grad),)
low.defvjp(low_keep, low_pass)
low_back.defvjp(back_keep, back_low)

def rms_scale(values):
    return lax.rsqrt(lax.optimization_barrier(jnp.mean(values * values, axis=-1, keepdims=True)) + eps_norm)

def norm_part(values, gain_vec):
    return values * rms_scale(values) * gain_vec

def rotate(values, cosine, sine_table):
    half_size = values.shape[-1] // 2
    turned = jnp.concatenate([-values[..., half_size:], values[..., :half_size]], axis=-1)
    return values * cosine + turned * sine_table

def angle_tables(positions, head_size):
    freq_index = jnp.arange(head_size // 2, dtype=jnp.float32)
    inverse = jnp.exp(freq_index * (-2.0 * math.log(theta_base) / head_size))
    angles = positions.astype(jnp.float32)[..., None] * inverse
    angles = jnp.concatenate([angles, angles], axis=-1)
    return (jnp.cos(angles), jnp.sin(angles))

def doc_layout(length_rows, positions):
    ends_sum = jnp.cumsum(length_rows, axis=-1, dtype=jnp.int32)
    passed = positions[None, :, None] >= ends_sum[:, None, :]
    doc_index = lax.optimization_barrier(jnp.sum(passed.astype(jnp.int32), axis=-1, dtype=jnp.int32))
    starts = lax.optimization_barrier(jnp.sum(jnp.where(passed, length_rows[:, None, :], 0), axis=-1, dtype=jnp.int32))
    return (doc_index, positions[None, :] - starts)

def matmul_high(left, right):
    return jnp.dot(left, right, precision=lax.Precision.HIGHEST, preferred_element_type=jnp.float32)

def block_forward(tokens, params, doc_index, inner_pos):
    gain_one, query_mat, key_mat, value_mat, gate_mat, out_mat, query_gain, key_gain, gain_two, gate_wide, up_wide, down_wide = params
    cosine, sine_table = angle_tables(inner_pos, HD)
    cosine = cosine[:, None, :]
    sine_table = sine_table[:, None, :]
    hidden_one = low(norm_part(tokens, gain_one))
    query_raw = low_back(matmul_high(hidden_one, query_mat)).reshape(BUCKET, H, HD)
    key_raw = low_back(matmul_high(hidden_one, key_mat)).reshape(BUCKET, KVH, HD)
    value_rows = low(low_back(matmul_high(hidden_one, value_mat))).reshape(BUCKET, KVH, HD)
    gate_raw = low_back(matmul_high(hidden_one, gate_mat))
    query_rot = low(rotate(norm_part(query_raw, query_gain), cosine, sine_table)).reshape(BUCKET, KVH, H // KVH, HD)
    key_rot = low(rotate(norm_part(key_raw, key_gain), cosine, sine_table))
    scores = low_back(jnp.einsum('qkgd,skd->kgqs', query_rot, key_rot, precision=lax.Precision.HIGHEST) * HD ** (-0.5))
    positions = jnp.arange(BUCKET, dtype=jnp.int32)
    allowed = (doc_index[:, None] == doc_index[None, :]) & (positions[None, :] <= positions[:, None])
    scores = jnp.where(allowed[None, None], scores, masked_score)
    row_peak = lax.optimization_barrier(jnp.max(scores, axis=-1, keepdims=True))
    shifted = jnp.exp(scores - row_peak)
    prob_rows = low(shifted / lax.optimization_barrier(jnp.sum(shifted, axis=-1, keepdims=True)))
    mixed_rows = low_back(jnp.einsum('kgqs,skd->qkgd', prob_rows, value_rows, precision=lax.Precision.HIGHEST)).reshape(BUCKET, H * HD)
    gated_rows = low(mixed_rows * jax.nn.sigmoid(gate_raw))
    residual = tokens + low_back(matmul_high(gated_rows, out_mat))
    hidden_two = low(norm_part(residual, gain_two))
    gate_pre = low_back(matmul_high(hidden_two, gate_wide))
    up_pre = low_back(matmul_high(hidden_two, up_wide))
    inner_act = low(jax.nn.silu(gate_pre) * up_pre)
    return residual + low_back(matmul_high(inner_act, down_wide))

def reference(block_input, doc_lengths, norm_attn, w_query, w_key, w_value, w_gate_attn, w_out, gain_query, gain_key, norm_ffn, w_gate, w_up, w_down, grad_output):
    weights = (norm_attn.astype(jnp.float32), w_query.astype(jnp.float32), w_key.astype(jnp.float32), w_value.astype(jnp.float32), w_gate_attn.astype(jnp.float32), w_out.astype(jnp.float32), gain_query.astype(jnp.float32), gain_key.astype(jnp.float32), norm_ffn.astype(jnp.float32), w_gate.astype(jnp.float32), w_up.astype(jnp.float32), w_down.astype(jnp.float32))
    bucket_total = MB * NSEQ
    flat_rows = block_input.astype(jnp.float32).reshape(bucket_total, BUCKET, D)
    flat_lengths = doc_lengths.reshape(bucket_total, NDOC)
    flat_cot = grad_output.astype(jnp.float32).reshape(bucket_total, BUCKET, D)
    positions = jnp.arange(BUCKET, dtype=jnp.int32)

    def bucket_step(running_sums, bucket_data):
        bucket_rows, bucket_lengths, bucket_cot = bucket_data
        doc_index, inner_pos = doc_layout(bucket_lengths[None, :], positions)

        def forward(rows_in, params):
            return block_forward(rows_in, params, doc_index[0], inner_pos[0])
        outputs, pullback = jax.vjp(forward, bucket_rows, weights)
        grad_rows, grad_params = pullback(bucket_cot)
        running_sums = tuple((running + addend for running, addend in zip(running_sums, grad_params)))
        return (running_sums, (outputs.astype(jnp.bfloat16), grad_rows))
    zero_grads = tuple((jnp.zeros(member.shape, jnp.float32) for member in weights))
    grad_sums, stacked = lax.scan(bucket_step, zero_grads, (flat_rows, flat_lengths, flat_cot))
    return (stacked[0].reshape(block_input.shape), stacked[1].reshape(block_input.shape), grad_sums[0], grad_sums[1], grad_sums[2], grad_sums[3], grad_sums[4], grad_sums[5], grad_sums[6], grad_sums[7], grad_sums[8], grad_sums[9], grad_sums[10], grad_sums[11])
```

```python
import functools
import math

import jax
import jax.numpy as jnp
from jax import lax
from jax.experimental import pallas as pl
from jax.experimental.pallas import tpu as pltpu
from jax.sharding import Mesh
from jax.sharding import PartitionSpec as P

f32 = jnp.float32
bf16 = jnp.bfloat16
eps_norm = 1e-06
theta_base = 1000000.0
masked_score = -1e30
plane = ("x", "c", "y")
swap = [(0, 1), (1, 0)]
cross = [(0, 3), (3, 0), (1, 2), (2, 1)]


def dot(a, b, ca, cb, out=f32):
    return lax.dot_general(a, b, (((ca,), (cb,)), ((), ())), preferred_element_type=f32).astype(out)


def send_c(v):
    return lax.ppermute(v, "c", swap)


def send_x(v):
    return lax.ppermute(v, "x", swap)


def send_y(v):
    return lax.ppermute(v, "y", swap)


def send_xy(v):
    return lax.ppermute(v, ("x", "y"), cross)


def gather_plane(v):
    own = jnp.concatenate([v, send_y(v), send_x(v), send_xy(v)], axis=0)
    return own, send_c(own)


def reduce_plane(own, other):
    total = own + send_c(other).astype(f32)
    rows = own.shape[0] // 4
    part = [total[i * rows : (i + 1) * rows] for i in range(4)]
    low = [p.astype(bf16) for p in part]
    got = (send_y(low[1]), send_x(low[2]), send_xy(low[3]))
    return part[0] + got[0].astype(f32) + got[1].astype(f32) + got[2].astype(f32)


def doubling(v, axis, count, join):
    step = 1
    while step < count:
        v = join(v, lax.ppermute(v, axis, [(i, i ^ step) for i in range(count)]), step)
        step *= 2
    return v


def gather_rows(v, axis):
    count = lax.axis_size(axis)
    index = lax.axis_index(axis)

    def join(mine, theirs, step):
        low = (index & step) == 0
        return jnp.where(
            low,
            jnp.concatenate([mine, theirs], axis=0),
            jnp.concatenate([theirs, mine], axis=0),
        )

    return doubling(v, axis, count, join)


def sum_all(v, axis):
    return doubling(v, axis, lax.axis_size(axis), lambda a, b, step: a + b)


def rms_scale(values):
    return lax.rsqrt(jnp.mean(values * values, axis=-1, keepdims=True) + eps_norm)


def norm_back(grad, values, scale, gain):
    weighted = grad * gain
    inner = jnp.mean(weighted * values, axis=-1, keepdims=True)
    return scale * (weighted - values * (scale * scale) * inner), grad * values * scale


def angle_tables(positions, head_size):
    freq_index = jnp.arange(head_size // 2, dtype=f32)
    inverse = jnp.exp(freq_index * (-2.0 * math.log(theta_base) / head_size))
    angles = positions.astype(f32)[..., None] * inverse
    cosine, sine = jnp.cos(angles), jnp.sin(angles)
    return jnp.concatenate([cosine, cosine], -1), jnp.concatenate([-sine, sine], -1)


def softmax_rows(query, key, allowed, scale):
    scores = lax.dot_general(query, key, (((1,), (1,)), ((), ())), preferred_element_type=f32) * scale
    scores = jnp.where(allowed, scores, masked_score)
    shifted = jnp.exp(scores - jnp.max(scores, axis=-1, keepdims=True))
    return shifted / jnp.sum(shifted, axis=-1, keepdims=True)


def turn(values, cosine, sine):
    half = values.shape[-1] // 2
    return values * cosine + pltpu.roll(values, half, 1) * sine


def turn_back(grad, cosine, sine):
    half = grad.shape[-1] // 2
    return grad * cosine - pltpu.roll(grad, half, 1) * sine


def sigmoid(v):
    return 1.0 / (1.0 + jnp.exp(-v))


def load_rows(ref, low, high):
    part = ref[0, :, 0, :, low:high]
    return part.reshape(part.shape[0] * part.shape[1], high - low)


def store_rows(ref, low, high, value):
    _, halves, _, rows, _ = ref.shape
    ref[0, :, 0, :, low:high] = value.reshape(halves, rows, high - low)


def forward_kernel(size, group, proj, cos, sin, mask, gains, gated):
    scale = size ** (-0.5)
    cosine, sine = load_rows(cos, 0, size), load_rows(sin, 0, size)
    allowed = mask[0, 0] > 0.0
    wide = group * size
    key_raw = load_rows(proj, wide, wide + size)
    key = turn(key_raw * rms_scale(key_raw) * gains[1:2, :], cosine, sine).astype(bf16)
    value = load_rows(proj, wide + size, wide + 2 * size).astype(bf16)
    for h in range(group):
        low, high = h * size, (h + 1) * size
        query_raw = load_rows(proj, low, high)
        query = turn(query_raw * rms_scale(query_raw) * gains[0:1, :], cosine, sine).astype(bf16)
        prob = softmax_rows(query, key, allowed, scale).astype(bf16)
        mixed = jnp.dot(prob, value, preferred_element_type=f32)
        gate = sigmoid(load_rows(proj, wide + 2 * size + low, wide + 2 * size + high))
        store_rows(gated, low, high, (mixed * gate).astype(bf16))


def backward_kernel(size, group, proj, grad, cos, sin, mask, gains, out, gain_out):
    scale = size ** (-0.5)
    cosine, sine = load_rows(cos, 0, size), load_rows(sin, 0, size)
    allowed = mask[0, 0] > 0.0
    wide = group * size
    gain_q, gain_k = gains[0:1, :], gains[1:2, :]
    key_raw = load_rows(proj, wide, wide + size)
    key_scale = rms_scale(key_raw)
    key = turn(key_raw * key_scale * gain_k, cosine, sine).astype(bf16)
    value = load_rows(proj, wide + size, wide + 2 * size).astype(bf16)
    grad_key = jnp.zeros(key_raw.shape, f32)
    grad_value = jnp.zeros(key_raw.shape, f32)
    sum_q = jnp.zeros((1, size), f32)
    for h in range(group):
        low, high = h * size, (h + 1) * size
        query_raw = load_rows(proj, low, high)
        query_scale = rms_scale(query_raw)
        query = turn(query_raw * query_scale * gain_q, cosine, sine).astype(bf16)
        prob = softmax_rows(query, key, allowed, scale)
        prob_low = prob.astype(bf16)
        mixed = jnp.dot(prob_low, value, preferred_element_type=f32)
        gate = sigmoid(load_rows(proj, wide + 2 * size + low, wide + 2 * size + high))
        incoming = load_rows(grad, low, high)
        grad_mixed = (incoming * gate).astype(bf16)
        grad_gate = (incoming * mixed * gate * (1.0 - gate)).astype(bf16)
        store_rows(out, wide + 2 * size + low, wide + 2 * size + high, grad_gate)
        grad_prob = lax.dot_general(
            grad_mixed, value, (((1,), (1,)), ((), ())), preferred_element_type=f32
        )
        centre = jnp.sum(prob * grad_prob, axis=-1, keepdims=True)
        grad_score = (prob * (grad_prob - centre)).astype(bf16)
        grad_query = jnp.dot(grad_score, key, preferred_element_type=f32) * scale
        grad_key += lax.dot_general(
            grad_score, query, (((0,), (0,)), ((), ())), preferred_element_type=f32
        )
        grad_value += lax.dot_general(
            prob_low, grad_mixed, (((0,), (0,)), ((), ())), preferred_element_type=f32
        )
        raw, addend = norm_back(turn_back(grad_query, cosine, sine), query_raw, query_scale, gain_q)
        sum_q += jnp.sum(addend, axis=0, keepdims=True)
        store_rows(out, low, high, raw.astype(bf16))
    raw, addend = norm_back(turn_back(grad_key * scale, cosine, sine), key_raw, key_scale, gain_k)
    store_rows(out, wide, wide + size, raw.astype(bf16))
    store_rows(out, wide + size, wide + 2 * size, grad_value.astype(bf16))
    gain_out[0, 0, 0:1, :] = sum_q
    gain_out[0, 0, 1:2, :] = jnp.sum(addend, axis=0, keepdims=True)


def rows_spec(micro, rows, width):
    return pl.BlockSpec((1, 2, 1, rows, width), lambda i, m: (i, 0, m, 0, 0))


def attention_forward(proj, tables, gains, group, micro):
    cos, sin, mask = tables
    rows, size = cos.shape[3], cos.shape[4]
    view = proj.reshape(2, 2, micro, rows, proj.shape[1])
    spec = functools.partial(rows_spec, micro, rows)
    out = pl.pallas_call(
        functools.partial(forward_kernel, size, group),
        grid=(2, micro),
        in_specs=[
            spec(proj.shape[1]),
            spec(size),
            spec(size),
            pl.BlockSpec((1, 1, 2 * rows, 2 * rows), lambda i, m: (i, m, 0, 0)),
            pl.BlockSpec((2, size), lambda i, m: (0, 0)),
        ],
        out_specs=spec(group * size),
        out_shape=jax.ShapeDtypeStruct((2, 2, micro, rows, group * size), bf16),
        name="attn_fwd",
    )(view, cos, sin, mask, gains)
    return out.reshape(proj.shape[0], group * size)


def attention_backward(proj, grad, tables, gains, group, micro):
    cos, sin, mask = tables
    rows, size = cos.shape[3], cos.shape[4]
    spec = functools.partial(rows_spec, micro, rows)
    out, sums = pl.pallas_call(
        functools.partial(backward_kernel, size, group),
        grid=(2, micro),
        in_specs=[
            spec(proj.shape[1]),
            spec(group * size),
            spec(size),
            spec(size),
            pl.BlockSpec((1, 1, 2 * rows, 2 * rows), lambda i, m: (i, m, 0, 0)),
            pl.BlockSpec((2, size), lambda i, m: (0, 0)),
        ],
        out_specs=[
            spec(proj.shape[1]),
            pl.BlockSpec((1, 1, 2, size), lambda i, m: (i, m, 0, 0)),
        ],
        out_shape=[
            jax.ShapeDtypeStruct((2, 2, micro, rows, proj.shape[1]), bf16),
            jax.ShapeDtypeStruct((2, micro, 2, size), f32),
        ],
        name="attn_bwd",
    )(
        proj.reshape(2, 2, micro, rows, proj.shape[1]),
        grad.reshape(2, 2, micro, rows, grad.shape[1]),
        cos,
        sin,
        mask,
        gains,
    )
    return out.reshape(proj.shape), jnp.sum(sums, axis=(0, 1))


def make_tables(lengths, side, rows, size):
    inner = jnp.arange(rows, dtype=jnp.int32)
    position = jnp.concatenate([side * rows + inner, (1 - side) * rows + inner])
    ends = jnp.cumsum(lengths, axis=-1, dtype=jnp.int32)
    passed = position[None, None, :, None] >= ends[:, :, None, :]
    doc = jnp.sum(passed.astype(jnp.int32), axis=-1, dtype=jnp.int32)
    starts = jnp.sum(jnp.where(passed, lengths[:, :, None, :], 0), axis=-1, dtype=jnp.int32)
    cos, sin = angle_tables(position - starts, size)
    mask = (doc[:, :, :, None] == doc[:, :, None, :]) & (position[None, :] <= position[:, None])

    def halves(v):
        return v.reshape(2, v.shape[1], 2, rows, size).transpose(0, 2, 1, 3, 4)

    return halves(cos), halves(sin), mask.astype(f32)


def pack_columns(mats):
    parts = [m.reshape(m.shape[0], 4, m.shape[1] // 4) for m in mats]
    return jnp.concatenate(parts, axis=2).transpose(1, 0, 2)


def share_columns(mats):
    packed = lax.all_to_all(pack_columns(mats), ("x", "c"), split_axis=0, concat_axis=0, tiled=True)
    packed = packed.reshape(packed.shape[0] * packed.shape[1], packed.shape[2])
    return lax.all_gather(packed, "g", axis=0, tiled=True)


def return_columns(grad, widths):
    mine = lax.psum_scatter(grad, "g", scatter_dimension=0, tiled=True)
    blocks = mine.reshape(4, mine.shape[0] // 4, mine.shape[1])
    got = lax.all_to_all(blocks, ("x", "c"), split_axis=0, concat_axis=0, tiled=True)
    outs, low = [], 0
    for width in widths:
        part = got[:, :, low : low + width].transpose(1, 0, 2)
        outs.append(part.reshape(part.shape[0], 4 * width).astype(f32))
        low += width
    return outs


def row_route(group_count, col_count):
    per = group_count // col_count
    pairs = []
    for f in range(4 * group_count):
        for y in range(col_count):
            block, inner = f // per, f % per
            target = inner * col_count + y
            y_to, rest = block // 4, block % 4
            pairs.append((f * col_count + y, (target * 4 + rest) * col_count + y_to))
    return pairs


every = ("g", "x", "c", "y")


def share_rows(mat, route, col_count):
    moved = lax.ppermute(mat, every, route)
    full = lax.all_gather(moved[None], "g", axis=0, tiled=True)
    count, rows, cols = full.shape
    full = full.reshape(count // col_count, col_count, rows, cols).transpose(0, 2, 1, 3)
    return full.reshape(count // col_count * rows, col_count * cols)


def return_rows(grad, route, group_count, col_count):
    per = group_count // col_count
    rows, cols = grad.shape[0] // per, grad.shape[1] // col_count
    blocks = grad.reshape(per, rows, col_count, cols).transpose(0, 2, 1, 3)
    blocks = blocks.reshape(group_count * rows, cols)
    mine = lax.psum_scatter(blocks, "g", scatter_dimension=0, tiled=True)
    return lax.ppermute(mine, every, [(b, a) for a, b in route]).astype(f32)


def body(
    block_input,
    doc_lengths,
    norm_attn,
    w_query,
    w_key,
    w_value,
    w_gate_attn,
    w_out,
    gain_query,
    gain_key,
    norm_ffn,
    w_gate,
    w_up,
    w_down,
    grad_output,
):
    group_count, col_count = lax.axis_size("g"), lax.axis_size("y")
    fsdp_count = 4 * group_count
    side = lax.axis_index("y")
    owner = lax.axis_index("g") * 4 + lax.axis_index("x") * 2 + lax.axis_index("c")
    micro, _, rows, width = block_input.shape
    size = gain_query.shape[0] * fsdp_count
    group = w_query.shape[1] // w_key.shape[1]
    route = row_route(group_count, col_count)

    tokens_low = block_input.reshape(micro * rows, width)
    cotangent = grad_output.reshape(micro * rows, width)

    token_pair = gather_plane(tokens_low)
    packed = jnp.concatenate([norm_attn, norm_ffn, gain_query, gain_key])[None]
    every_gain = gather_rows(gather_rows(gather_rows(packed, "c"), "x"), "g").astype(f32)
    piece, small = norm_attn.shape[0], gain_query.shape[0]
    gain_one = every_gain[:, :piece].reshape(1, width)
    gain_two = every_gain[:, piece : 2 * piece].reshape(1, width)
    gain_q = every_gain[:, 2 * piece : 2 * piece + small].reshape(1, size)
    gain_k = every_gain[:, 2 * piece + small :].reshape(1, size)
    head_gains = jnp.concatenate([gain_q, gain_k], axis=0)
    lengths = doc_lengths.reshape(1, micro, doc_lengths.shape[2])
    lengths = jnp.concatenate([lengths, send_x(lengths)], axis=0)
    tables = [make_tables(v, side, rows, size) for v in (lengths, send_c(lengths))]

    qkvg = share_columns((w_query, w_key, w_value, w_gate_attn))
    out_rows = share_rows(w_out, route, col_count)
    gate_up = share_columns((w_gate, w_up))
    down_rows = share_rows(w_down, route, col_count)
    cot_pair = gather_plane(cotangent)

    def first_norm(v):
        v = v.astype(f32)
        return (v * rms_scale(v) * gain_one).astype(bf16)

    hidden = [first_norm(v) for v in token_pair]
    proj = [dot(h, qkvg, 1, 0) for h in hidden]
    gated = [attention_forward(p, t, head_gains, group, micro) for p, t in zip(proj, tables)]
    mixed = reduce_plane(dot(gated[0], out_rows, 1, 0), dot(gated[1], out_rows, 1, 0, bf16))
    tokens = tokens_low.astype(f32)
    residual = tokens + mixed
    scale_two = rms_scale(residual)
    hidden_two = gather_plane((residual * scale_two * gain_two).astype(bf16))
    units = gate_up.shape[1] // 2

    inner, grad_units = [], []
    for h, g in zip(hidden_two, cot_pair):
        pre = dot(h, gate_up, 1, 0)
        gate_pre, up_pre = pre[:, :units], pre[:, units:]
        grad_inner = dot(g, down_rows, 1, 1)
        sig = jax.nn.sigmoid(gate_pre)
        act = gate_pre * sig
        inner.append((act * up_pre).astype(bf16))
        grad_gate = grad_inner * up_pre * (sig * (1.0 + gate_pre * (1.0 - sig)))
        grad_units.append(
            jnp.concatenate([grad_gate.astype(bf16), (grad_inner * act).astype(bf16)], axis=1)
        )
    grad_hidden_two = reduce_plane(
        dot(grad_units[0], gate_up, 1, 1), dot(grad_units[1], gate_up, 1, 1, bf16)
    )
    final = reduce_plane(dot(inner[0], down_rows, 1, 0), dot(inner[1], down_rows, 1, 0, bf16))
    block_output = (residual + final).astype(bf16).reshape(block_input.shape)

    def weight_grad(left, right):
        return (dot(left[0], right[0], 0, 0) + dot(left[1], right[1], 0, 0)).astype(bf16)

    grad_down = return_rows(weight_grad(inner, cot_pair), route, group_count, col_count)
    grad_gate, grad_up = return_columns(
        weight_grad(hidden_two, grad_units), (units, units)
    )

    back, addend = norm_back(grad_hidden_two, residual, scale_two, gain_two)
    sum_two = jnp.sum(addend, axis=0)
    grad_resid = cotangent.astype(f32) + back
    low_pair = gather_plane(grad_resid.astype(bf16))
    grad_gated = [dot(d, out_rows, 1, 1) for d in low_pair]
    backs = [
        attention_backward(p, d, t, head_gains, group, micro)
        for p, d, t in zip(proj, grad_gated, tables)
    ]
    grad_proj = [b[0] for b in backs]
    grad_hidden = reduce_plane(dot(grad_proj[0], qkvg, 1, 1), dot(grad_proj[1], qkvg, 1, 1, bf16))
    grad_out = return_rows(weight_grad(gated, low_pair), route, group_count, col_count)
    query_width, key_width = group * size, size
    grad_query, grad_key, grad_value, grad_gate_attn = return_columns(
        weight_grad(hidden, grad_proj), (query_width, key_width, key_width, query_width)
    )
    back, addend = norm_back(grad_hidden, tokens, rms_scale(tokens), gain_one)
    grad_input = (grad_resid + back).reshape(block_input.shape)

    head_sums = backs[0][1] + backs[1][1]
    sums = jnp.concatenate(
        [
            jnp.sum(addend, axis=0).reshape(fsdp_count, piece),
            sum_two.reshape(fsdp_count, piece),
            head_sums[0].reshape(fsdp_count, small),
            head_sums[1].reshape(fsdp_count, small),
        ],
        axis=1,
    )
    for axis in ("c", "y", "x", "g"):
        sums = sum_all(sums, axis)
    mine = lax.dynamic_index_in_dim(sums, owner, 0, keepdims=False)
    return (
        block_output,
        grad_input,
        mine[:piece],
        grad_query,
        grad_key,
        grad_value,
        grad_gate_attn,
        grad_out,
        mine[2 * piece : 2 * piece + small],
        mine[2 * piece + small :],
        mine[piece : 2 * piece],
        grad_gate,
        grad_up,
        grad_down,
    )


def solution(mesh):
    fsdp_count, col_count = mesh.shape["fsdp"], mesh.shape["col"]
    grid = Mesh(mesh.devices.reshape(fsdp_count // 4, 2, 2, col_count), every)
    rows = ("g", "x", "c")
    token, vector, matrix = P(None, rows, "y", None), P(rows), P(rows, "y")
    in_specs = (
        (token, P(None, rows, None), vector)
        + (matrix,) * 5
        + (vector,) * 3
        + (matrix,) * 3
        + (token,)
    )
    out_specs = (token, token, vector) + (matrix,) * 5 + (vector,) * 3 + (matrix,) * 3
    return jax.shard_map(body, mesh=grid, in_specs=in_specs, out_specs=out_specs, check_vma=False)
```

```python
import functools
import math

import jax
import jax.numpy as jnp
from jax import lax
from jax.experimental import pallas as pl
from jax.experimental.pallas import tpu as pltpu
from jax.sharding import Mesh
from jax.sharding import PartitionSpec as P


f32 = jnp.float32
bf16 = jnp.bfloat16
eps_norm = 1e-06
theta_base = 1000000.0
masked_score = -1e30
data = ("h", "g")
swap = [(0, 1), (1, 0)]
cross = [(0, 3), (3, 0), (1, 2), (2, 1)]


def dot(a, b, ca, cb, out=f32):
    return lax.dot_general(a, b, (((ca,), (cb,)), ((), ())), preferred_element_type=f32).astype(out)


def send_c(v):
    return lax.ppermute(v, "c", swap)


def send_plane(y, x, xy):
    return (
        lax.ppermute(y, "y", swap),
        lax.ppermute(x, "x", swap),
        lax.ppermute(xy, ("x", "y"), cross),
    )


def send_mirror(v):
    count = lax.axis_size("h") * lax.axis_size("g")
    return lax.ppermute(v, data, [(i, count - 1 - i) for i in range(count)])


def after(value, *others):
    return lax.optimization_barrier((value, *others))[0]


def gather_plane(v, *others):
    own = jnp.concatenate([v, *send_plane(v, v, v)], axis=0)
    return own, send_c(after(own, *others))


def fold_cores(own, other):
    theirs = send_c(other)
    total = own + theirs.astype(f32)
    rows = own.shape[0] // 4
    part = [total[i * rows : (i + 1) * rows] for i in range(4)]
    return part[0], [p.astype(bf16) for p in part[1:]]


def finish(own, low):
    got = send_plane(*low)
    return own + got[0].astype(f32) + got[1].astype(f32) + got[2].astype(f32)


def finish_pair(near, far):
    moved = send_mirror(finish(*far).astype(bf16))
    return finish(*near) + moved.astype(f32)


def rms_scale(values):
    return lax.rsqrt(jnp.mean(values * values, axis=-1, keepdims=True) + eps_norm)


def norm_back(grad, values, scale, gain):
    weighted = grad * gain
    inner = jnp.mean(weighted * values, axis=-1, keepdims=True)
    return scale * (weighted - values * (scale * scale) * inner), grad * values * scale


def angle_tables(positions, head_size):
    freq_index = jnp.arange(head_size // 2, dtype=f32)
    inverse = jnp.exp(freq_index * (-2.0 * math.log(theta_base) / head_size))
    angles = positions.astype(f32)[..., None] * inverse
    cosine, sine = jnp.cos(angles), jnp.sin(angles)
    return jnp.concatenate([cosine, cosine], -1), jnp.concatenate([-sine, sine], -1)


def softmax_rows(query, key, allowed, scale):
    scores = lax.dot_general(query, key, (((1,), (1,)), ((), ())), preferred_element_type=f32) * scale
    scores = jnp.where(allowed, scores, masked_score)
    shifted = jnp.exp(scores - jnp.max(scores, axis=-1, keepdims=True))
    return shifted / jnp.sum(shifted, axis=-1, keepdims=True)


def turn(values, cosine, sine):
    half = values.shape[-1] // 2
    return values * cosine + pltpu.roll(values, half, 1) * sine


def turn_back(grad, cosine, sine):
    half = grad.shape[-1] // 2
    return grad * cosine - pltpu.roll(grad, half, 1) * sine


def sigmoid(v):
    return 1.0 / (1.0 + jnp.exp(-v))


def load_rows(ref, low, high):
    part = ref[0, :, 0, :, low:high]
    return part.reshape(part.shape[0] * part.shape[1], high - low)


def store_rows(ref, low, high, value):
    _, halves, _, rows, _ = ref.shape
    ref[0, :, 0, :, low:high] = value.reshape(halves, rows, high - low)


def forward_kernel(size, group, proj, cos, sin, mask, gains, gated):
    scale = size ** (-0.5)
    cosine, sine = load_rows(cos, 0, size), load_rows(sin, 0, size)
    allowed = mask[0, 0] > 0.0
    wide = group * size
    key_raw = load_rows(proj, wide, wide + size)
    key = turn(key_raw * rms_scale(key_raw) * gains[1:2, :], cosine, sine).astype(bf16)
    value = load_rows(proj, wide + size, wide + 2 * size).astype(bf16)
    for h in range(group):
        low, high = h * size, (h + 1) * size
        query_raw = load_rows(proj, low, high)
        query = turn(query_raw * rms_scale(query_raw) * gains[0:1, :], cosine, sine).astype(bf16)
        prob = softmax_rows(query, key, allowed, scale).astype(bf16)
        mixed = jnp.dot(prob, value, preferred_element_type=f32)
        gate = sigmoid(load_rows(proj, wide + 2 * size + low, wide + 2 * size + high))
        store_rows(gated, low, high, (mixed * gate).astype(bf16))


def backward_kernel(size, group, proj, grad, cos, sin, mask, gains, out, gain_out):
    scale = size ** (-0.5)
    cosine, sine = load_rows(cos, 0, size), load_rows(sin, 0, size)
    allowed = mask[0, 0] > 0.0
    wide = group * size
    gain_q, gain_k = gains[0:1, :], gains[1:2, :]
    key_raw = load_rows(proj, wide, wide + size)
    key_scale = rms_scale(key_raw)
    key = turn(key_raw * key_scale * gain_k, cosine, sine).astype(bf16)
    value = load_rows(proj, wide + size, wide + 2 * size).astype(bf16)
    grad_key = jnp.zeros(key_raw.shape, f32)
    grad_value = jnp.zeros(key_raw.shape, f32)
    sum_q = jnp.zeros((1, size), f32)
    for h in range(group):
        low, high = h * size, (h + 1) * size
        query_raw = load_rows(proj, low, high)
        query_scale = rms_scale(query_raw)
        query = turn(query_raw * query_scale * gain_q, cosine, sine).astype(bf16)
        prob = softmax_rows(query, key, allowed, scale)
        prob_low = prob.astype(bf16)
        mixed = jnp.dot(prob_low, value, preferred_element_type=f32)
        gate = sigmoid(load_rows(proj, wide + 2 * size + low, wide + 2 * size + high))
        incoming = load_rows(grad, low, high)
        grad_mixed = (incoming * gate).astype(bf16)
        grad_gate = (incoming * mixed * gate * (1.0 - gate)).astype(bf16)
        store_rows(out, wide + 2 * size + low, wide + 2 * size + high, grad_gate)
        grad_prob = lax.dot_general(
            grad_mixed, value, (((1,), (1,)), ((), ())), preferred_element_type=f32
        )
        centre = jnp.sum(prob * grad_prob, axis=-1, keepdims=True)
        grad_score = (prob * (grad_prob - centre)).astype(bf16)
        grad_query = jnp.dot(grad_score, key, preferred_element_type=f32) * scale
        grad_key += lax.dot_general(
            grad_score, query, (((0,), (0,)), ((), ())), preferred_element_type=f32
        )
        grad_value += lax.dot_general(
            prob_low, grad_mixed, (((0,), (0,)), ((), ())), preferred_element_type=f32
        )
        raw, addend = norm_back(turn_back(grad_query, cosine, sine), query_raw, query_scale, gain_q)
        sum_q += jnp.sum(addend, axis=0, keepdims=True)
        store_rows(out, low, high, raw.astype(bf16))
    raw, addend = norm_back(turn_back(grad_key * scale, cosine, sine), key_raw, key_scale, gain_k)
    store_rows(out, wide, wide + size, raw.astype(bf16))
    store_rows(out, wide + size, wide + 2 * size, grad_value.astype(bf16))
    gain_out[0, 0, 0:1, :] = sum_q
    gain_out[0, 0, 1:2, :] = jnp.sum(addend, axis=0, keepdims=True)


def rows_spec(rows, width):
    return pl.BlockSpec((1, 2, 1, rows, width), lambda i, m: (i, 0, m, 0, 0))


def attention_forward(proj, tables, gains, group, micro):
    cos, sin, mask = tables
    rows, size = cos.shape[3], cos.shape[4]
    view = proj.reshape(2, 2, micro, rows, proj.shape[1])
    spec = functools.partial(rows_spec, rows)
    out = pl.pallas_call(
        functools.partial(forward_kernel, size, group),
        grid=(2, micro),
        in_specs=[
            spec(proj.shape[1]),
            spec(size),
            spec(size),
            pl.BlockSpec((1, 1, 2 * rows, 2 * rows), lambda i, m: (i, m, 0, 0)),
            pl.BlockSpec((2, size), lambda i, m: (0, 0)),
        ],
        out_specs=spec(group * size),
        out_shape=jax.ShapeDtypeStruct((2, 2, micro, rows, group * size), bf16),
        name="attn_fwd",
    )(view, cos, sin, mask, gains)
    return out.reshape(proj.shape[0], group * size)


def attention_backward(proj, grad, tables, gains, group, micro):
    cos, sin, mask = tables
    rows, size = cos.shape[3], cos.shape[4]
    spec = functools.partial(rows_spec, rows)
    out, sums = pl.pallas_call(
        functools.partial(backward_kernel, size, group),
        grid=(2, micro),
        in_specs=[
            spec(proj.shape[1]),
            spec(group * size),
            spec(size),
            spec(size),
            pl.BlockSpec((1, 1, 2 * rows, 2 * rows), lambda i, m: (i, m, 0, 0)),
            pl.BlockSpec((2, size), lambda i, m: (0, 0)),
        ],
        out_specs=[
            spec(proj.shape[1]),
            pl.BlockSpec((1, 1, 2, size), lambda i, m: (i, m, 0, 0)),
        ],
        out_shape=[
            jax.ShapeDtypeStruct((2, 2, micro, rows, proj.shape[1]), bf16),
            jax.ShapeDtypeStruct((2, micro, 2, size), f32),
        ],
        name="attn_bwd",
    )(
        proj.reshape(2, 2, micro, rows, proj.shape[1]),
        grad.reshape(2, 2, micro, rows, grad.shape[1]),
        cos,
        sin,
        mask,
        gains,
    )
    return out.reshape(proj.shape), jnp.sum(sums, axis=(0, 1))


def make_tables(lengths, side, rows, size):
    inner = jnp.arange(rows, dtype=jnp.int32)
    position = jnp.concatenate([side * rows + inner, (1 - side) * rows + inner])
    ends = jnp.cumsum(lengths, axis=-1, dtype=jnp.int32)
    passed = position[None, None, :, None] >= ends[:, :, None, :]
    doc = jnp.sum(passed.astype(jnp.int32), axis=-1, dtype=jnp.int32)
    starts = jnp.sum(jnp.where(passed, lengths[:, :, None, :], 0), axis=-1, dtype=jnp.int32)
    cos, sin = angle_tables(position - starts, size)
    mask = (doc[:, :, :, None] == doc[:, :, None, :]) & (position[None, :] <= position[:, None])

    def halves(v):
        return v.reshape(2, v.shape[1], 2, rows, size).transpose(0, 2, 1, 3, 4)

    return halves(cos), halves(sin), mask.astype(f32)


def pack_kernel(count, *refs):
    *mats, out = refs
    low = 0
    for mat in mats:
        wide = mat.shape[1] // count
        for i in range(count):
            out[0, i, :, low : low + wide] = mat[:, i * wide : (i + 1) * wide]
        low += wide


def pack_columns(mats, count, copies):
    rows, width = mats[0].shape[0], sum(m.shape[1] for m in mats) // count
    out = pl.pallas_call(
        functools.partial(pack_kernel, count),
        grid=(copies,),
        in_specs=[pl.BlockSpec(m.shape, lambda i: (0, 0)) for m in mats],
        out_specs=pl.BlockSpec((1, count, rows, width), lambda i: (i, 0, 0, 0)),
        out_shape=jax.ShapeDtypeStruct((copies, count, rows, width), mats[0].dtype),
        name="pack_columns",
    )(*mats)
    return out.reshape(copies * count, rows, width)


def unpack_kernel(widths, got, *outs):
    copies, count = got.shape[:2]
    for i in range(count):
        total = got[0, i].astype(f32)
        for j in range(1, copies):
            total = total + got[j, i].astype(f32)
        low = 0
        for width, out in zip(widths, outs):
            out[:, i * width : (i + 1) * width] = total[:, low : low + width]
            low += width


def unpack_columns(got, count, widths):
    copies, rows = got.shape[0] // count, got.shape[1]
    step = min(rows, 32)
    return pl.pallas_call(
        functools.partial(unpack_kernel, widths),
        grid=(rows // step,),
        in_specs=[pl.BlockSpec((copies, count, step, got.shape[2]), lambda i: (0, 0, i, 0))],
        out_specs=[pl.BlockSpec((step, count * w), lambda i: (i, 0)) for w in widths],
        out_shape=[jax.ShapeDtypeStruct((rows, count * w), f32) for w in widths],
        name="unpack_columns",
    )(got.reshape(copies, count, rows, got.shape[2]))


def exchange(blocks, axes):
    return lax.all_to_all(blocks, axes, split_axis=0, concat_axis=0, tiled=True)


def collect(mine, axes, axis):
    return lax.all_gather(mine, axes, axis=axis, tiled=True)


def scatter(full, axes, axis):
    return lax.psum_scatter(full, axes, scatter_dimension=axis, tiled=True)


def route_by(v, pairs):
    return lax.ppermute(v, every, pairs)


every = ("h", "g", "x", "c", "y")


def row_route(ranks, fsdp_count, col_count):
    per = fsdp_count // (ranks * col_count)
    planes = fsdp_count // 4
    pairs = []
    for f in range(fsdp_count):
        for y in range(col_count):
            block, inner = f // per, f % per
            y_to, rest = block // ranks, block % ranks
            plane = inner * col_count + y + rest // 4 * (planes // 2)
            pairs.append((f * col_count + y, (plane * 4 + rest % 4) * col_count + y_to))
    return pairs


def join_rows(full, col_count):
    count, rows, cols = full.shape
    full = full.reshape(count // col_count, col_count, rows, cols).transpose(0, 2, 1, 3)
    return full.reshape(count // col_count * rows, col_count * cols)


def return_rows(grad, axes, route, col_count):
    count = lax.axis_size(axes)
    rows, cols = grad.shape[0] // (count // col_count), grad.shape[1] // col_count
    blocks = [
        grad[i // col_count * rows :, i % col_count * cols :][:rows, :cols] for i in range(count)
    ]
    mine = scatter(jnp.concatenate(blocks), axes, 0)
    return route_by(mine, [(b, a) for a, b in route]).astype(f32)


def inner_body(
    block_input,
    doc_lengths,
    norm_attn,
    w_query,
    w_key,
    w_value,
    w_gate_attn,
    w_out,
    gain_query,
    gain_key,
    norm_ffn,
    w_gate,
    w_up,
    w_down,
    grad_output,
):
    col_count = lax.axis_size("y")
    fsdp_count = 4 * lax.axis_size(data)
    side = lax.axis_index("y")
    micro, _, rows, width = block_input.shape
    size = gain_query.shape[0] * fsdp_count
    group = w_query.shape[1] // w_key.shape[1]
    shards, near, wide = ("h", "g", "x", "c"), ("x", "c"), ("h", "x", "c")
    plane_count = fsdp_count // 4
    route_out = row_route(4, fsdp_count, col_count)
    route_down = row_route(8, fsdp_count, col_count)

    tokens_low = block_input.reshape(micro * rows, width)
    cotangent = grad_output.reshape(micro * rows, width)

    flat = doc_lengths.reshape(-1)
    packed = jnp.concatenate([norm_attn, norm_ffn, gain_query, gain_key, flat.astype(bf16)])
    packed = jnp.broadcast_to(packed, (fsdp_count, packed.shape[0]))
    every_gain = exchange(packed, shards).astype(f32)
    every_length = every_gain[:, -flat.shape[0] :].astype(jnp.int32)
    owner = lax.axis_index(shards)
    piece, small = norm_attn.shape[0], gain_query.shape[0]
    gain_one = every_gain[:, :piece].reshape(1, width)
    gain_two = every_gain[:, piece : 2 * piece].reshape(1, width)
    gain_q = every_gain[:, 2 * piece : 2 * piece + small].reshape(1, size)
    gain_k = every_gain[:, 2 * piece + small : 2 * piece + 2 * small].reshape(1, size)
    head_gains = jnp.concatenate([gain_q, gain_k], axis=0)

    def lengths_of(core):
        picked = [every_length[owner ^ core], every_length[owner ^ core ^ 2]]
        return jnp.stack(picked).reshape(2, micro, doc_lengths.shape[2])

    tables = [make_tables(lengths_of(core), side, rows, size) for core in (0, 1)]

    packed_wide = pack_columns((w_gate, w_up), 8, 1)
    packed = pack_columns((w_query, w_key, w_value, w_gate_attn), 4, 1)
    moved = route_by(w_out, route_out)
    spread = exchange(packed, near)
    cut = moved.shape[1] // 4
    moved = jnp.stack([moved[:, i * cut : (i + 1) * cut] for i in range(4)])
    if moved.shape[1] == spread.shape[1]:
        full = collect(jnp.concatenate([spread, moved], axis=2), data, 0)
        full = full.reshape(plane_count, 4, *full.shape[1:])
        qkvg, full = full[..., : spread.shape[2]], full[..., spread.shape[2] :]
    else:
        qkvg = collect(spread, data, 0)
        full = collect(moved[None], data, 0)
    qkvg = qkvg.reshape(width, spread.shape[2])
    full = full.reshape(plane_count // col_count, col_count, 4, moved.shape[1], cut)
    out_rows = full.transpose(0, 3, 1, 2, 4).reshape(-1, col_count * 4 * cut)
    token_pair = gather_plane(after(tokens_low, spread), packed_wide)
    cot_list = gather_plane(after(cotangent, token_pair[0]))
    moved = route_by(after(w_down, token_pair[0]), route_down)
    down_rows = join_rows(collect(moved[None], "g", 0), col_count)
    far = send_mirror(after(cotangent, token_pair[0]))
    cot_list += gather_plane(after(far, cot_list[0]))
    spread = exchange(after(packed_wide, cot_list[0], far), wide)
    gate_up = collect(spread.reshape(2, -1, spread.shape[2]), "g", 1)
    gate_up = gate_up.reshape(-1, spread.shape[2])

    def first_norm(v):
        v = v.astype(f32)
        return (v * rms_scale(v) * gain_one).astype(bf16)

    def first_part(v, table):
        h = first_norm(v)
        p = dot(h, qkvg, 1, 0)
        return h, p, attention_forward(p, table, head_gains, group, micro)

    other = first_part(token_pair[1], tables[1])
    mine = first_part(after(token_pair[0], other[2]), tables[0])
    hidden, proj, gated = zip(mine, other)
    mixed = fold_cores(dot(gated[0], out_rows, 1, 0), dot(gated[1], out_rows, 1, 0, bf16))
    mixed = finish(*mixed)
    tokens = tokens_low.astype(f32)
    residual = tokens + mixed
    scale_two = rms_scale(residual)
    low = (residual * scale_two * gain_two).astype(bf16)
    far = send_mirror(low)
    hidden_two = gather_plane(low)
    hidden_two += gather_plane(after(far, hidden_two[0]))
    units = gate_up.shape[1] // 2

    inner, grad_units = [], []

    def feed(h, g):
        pre = dot(h, gate_up, 1, 0)
        gate_pre, up_pre = pre[:, :units], pre[:, units:]
        grad_inner = dot(g, down_rows, 1, 1)
        sig = jax.nn.sigmoid(gate_pre)
        act = gate_pre * sig
        zz = (act * up_pre).astype(bf16)
        grad_gate = grad_inner * up_pre * (sig * (1.0 + gate_pre * (1.0 - sig)))
        pair = [grad_gate.astype(bf16), (grad_inner * act).astype(bf16)]
        return zz, jnp.concatenate(pair, axis=1)

    for i in range(4):
        zz, pair = feed(hidden_two[i], cot_list[i])
        inner.append(zz)
        grad_units.append(pair)

    def products(left, right, dim):
        kinds = (f32, bf16, f32, bf16)
        parts = [dot(v, right, 1, dim, kind) for v, kind in zip(left, kinds)]
        return parts[:2], parts[2:]

    def weight_grad(left, right):
        total = dot(left[0], right[0], 0, 0)
        for a, b in zip(left[1:], right[1:]):
            total = total + dot(a, b, 0, 0)
        return total.astype(bf16)

    near_parts, far_parts = products(grad_units, gate_up, 1)
    far_parts, near_parts = fold_cores(*far_parts), fold_cores(*near_parts)
    held = lax.optimization_barrier((*inner, *grad_units, *near_parts[1], *far_parts[1]))
    held_inner, held_units = held[:4], held[4:8]
    sum_units = weight_grad(hidden_two, held_units)
    mine = scatter(sum_units.reshape(2, width // 2, 2 * units), "g", 1)
    final_parts = products(held_inner, down_rows, 0)
    held = lax.optimization_barrier((*final_parts[0], *final_parts[1]))
    final_parts = fold_cores(*held[:2]), fold_cores(*held[2:])
    sum_down = weight_grad(held_inner, cot_list)
    grad_hidden_two = after(finish_pair(near_parts, far_parts), sum_down, sum_units)

    back, addend = norm_back(grad_hidden_two, residual, scale_two, gain_two)
    sum_two = jnp.sum(addend, axis=0)
    grad_resid = cotangent.astype(f32) + back
    low = grad_resid.astype(bf16)
    low_pair = gather_plane(low)
    got = exchange(mine.reshape(8, mine.shape[1] // 4, mine.shape[2]), wide)
    grad_gate, grad_up = unpack_columns(got, 8, (units, units))
    grad_down = return_rows(sum_down, "g", route_down, col_count)
    sum_out = weight_grad(gated, low_pair)
    grad_out = return_rows(sum_out, data, route_out, col_count)
    held = lax.optimization_barrier((*low_pair, sum_out))[:2]
    final = finish_pair(*final_parts)
    block_output = (residual + final).astype(bf16).reshape(block_input.shape)
    grad_gated = [dot(d, out_rows, 1, 1) for d in held]

    def attention_part(i):
        return attention_backward(proj[i], grad_gated[i], tables[i], head_gains, group, micro)

    backs = [attention_part(0), attention_part(1)]
    grad_proj = [b[0] for b in backs]
    sum_proj = weight_grad(hidden, grad_proj)
    got = exchange(sum_proj.reshape(fsdp_count, -1, sum_proj.shape[1]), shards)
    query_width, key_width = group * size, size
    grad_query, grad_key, grad_value, grad_gate_attn = unpack_columns(
        got, 4, (query_width, key_width, key_width, query_width)
    )
    grad_proj = lax.optimization_barrier((*grad_proj, sum_proj, block_output))[:2]
    parts = dot(grad_proj[0], qkvg, 1, 1), dot(grad_proj[1], qkvg, 1, 1, bf16)
    grad_hidden = finish(*fold_cores(*parts))
    back, addend = norm_back(grad_hidden, tokens, rms_scale(tokens), gain_one)
    grad_input = (grad_resid + back).reshape(block_input.shape)

    head_sums = backs[0][1] + backs[1][1]
    sums = jnp.concatenate(
        [
            jnp.sum(addend, axis=0).reshape(fsdp_count, piece),
            sum_two.reshape(fsdp_count, piece),
            head_sums[0].reshape(fsdp_count, small),
            head_sums[1].reshape(fsdp_count, small),
        ],
        axis=1,
    )
    mine = jnp.sum(exchange(after(sums, got), shards), axis=0)
    mine = mine + lax.ppermute(mine, "y", swap)
    return (
        block_output,
        grad_input,
        mine[:piece],
        grad_query,
        grad_key,
        grad_value,
        grad_gate_attn,
        grad_out,
        mine[2 * piece : 2 * piece + small],
        mine[2 * piece + small :],
        mine[piece : 2 * piece],
        grad_gate,
        grad_up,
        grad_down,
    )


def solution(mesh):
    fsdp_count, col_count = mesh.shape["fsdp"], mesh.shape["col"]
    grid = Mesh(mesh.devices.reshape(2, fsdp_count // 8, 2, 2, col_count), every)
    rows = ("h", "g", "x", "c")
    token, vector, matrix = P(None, rows, "y", None), P(rows), P(rows, "y")
    in_specs = (
        (token, P(None, rows, None), vector)
        + (matrix,) * 5
        + (vector,) * 3
        + (matrix,) * 3
        + (token,)
    )
    out_specs = (token, token, vector) + (matrix,) * 5 + (vector,) * 3 + (matrix,) * 3
    return jax.shard_map(inner_body, mesh=grid, in_specs=in_specs, out_specs=out_specs, check_vma=False)
```

```python
import functools
import math

import jax
import jax.numpy as jnp
from jax import lax
from jax.experimental import pallas as pl
from jax.experimental.pallas import tpu as pltpu
from jax.sharding import Mesh
from jax.sharding import PartitionSpec as P


f32 = jnp.float32
bf16 = jnp.bfloat16
eps_norm = 1e-06
theta_base = 1000000.0
masked_score = -1e30
data = ("h", "g")
swap = [(0, 1), (1, 0)]
cross = [(0, 3), (3, 0), (1, 2), (2, 1)]


def dot(a, b, ca, cb, out=f32):
    return lax.dot_general(a, b, (((ca,), (cb,)), ((), ())), preferred_element_type=f32).astype(out)


def send_c(v):
    return lax.ppermute(v, "c", swap)


def send_plane(y, x, xy):
    return (
        lax.ppermute(y, "y", swap),
        lax.ppermute(x, "x", swap),
        lax.ppermute(xy, ("x", "y"), cross),
    )


def send_mirror(v):
    count = lax.axis_size("h") * lax.axis_size("g")
    return lax.ppermute(v, data, [(i, count - 1 - i) for i in range(count)])


def after(value, *others):
    return lax.optimization_barrier((value, *others))[0]


def gather_plane(v, *others):
    own = jnp.concatenate([v, *send_plane(v, v, v)], axis=0)
    return own, send_c(after(own, *others))


def fold_cores(own, other):
    theirs = send_c(other)
    rows = own.shape[0] // 4
    total = own + theirs.astype(f32)
    low = [total[i * rows : (i + 1) * rows].astype(bf16) for i in range(1, 4)]
    return total[:rows], low


def finish(own, low):
    got = send_plane(*low)
    return own + got[0].astype(f32) + got[1].astype(f32) + got[2].astype(f32)


def finish_pair(near, far):
    moved = send_mirror(finish(*far).astype(bf16))
    return finish(*near) + moved.astype(f32)


def rms_scale(values):
    return lax.rsqrt(jnp.mean(values * values, axis=-1, keepdims=True) + eps_norm)


def norm_back(grad, values, scale, gain):
    weighted = grad * gain
    inner = jnp.mean(weighted * values, axis=-1, keepdims=True)
    return scale * (weighted - values * (scale * scale) * inner), grad * values * scale


def angle_tables(positions, head_size):
    freq_index = jnp.arange(head_size // 2, dtype=f32)
    inverse = jnp.exp(freq_index * (-2.0 * math.log(theta_base) / head_size))
    angles = positions.astype(f32)[..., None] * inverse
    cosine, sine = jnp.cos(angles), jnp.sin(angles)
    return jnp.concatenate([cosine, cosine], -1), jnp.concatenate([-sine, sine], -1)


def softmax_rows(query, key, allowed, scale):
    scores = lax.dot_general(query, key, (((1,), (1,)), ((), ())), preferred_element_type=f32) * scale
    scores = jnp.where(allowed, scores, masked_score)
    shifted = jnp.exp(scores - jnp.max(scores, axis=-1, keepdims=True))
    return shifted / jnp.sum(shifted, axis=-1, keepdims=True)


def turn(values, cosine, sine):
    half = values.shape[-1] // 2
    return values * cosine + pltpu.roll(values, half, 1) * sine


def turn_back(grad, cosine, sine):
    half = grad.shape[-1] // 2
    return grad * cosine - pltpu.roll(grad, half, 1) * sine


def sigmoid(v):
    return 1.0 / (1.0 + jnp.exp(-v))


def load_rows(ref, low, high):
    part = ref[0, :, 0, :, low:high]
    return part.reshape(part.shape[0] * part.shape[1], high - low)


def store_rows(ref, low, high, value):
    _, halves, _, rows, _ = ref.shape
    ref[0, :, 0, :, low:high] = value.reshape(halves, rows, high - low)


def forward_kernel(size, group, proj, cos, sin, mask, gains, gated):
    scale = size ** (-0.5)
    cosine, sine = load_rows(cos, 0, size), load_rows(sin, 0, size)
    allowed = mask[0, 0] > 0.0
    wide = group * size
    key_raw = load_rows(proj, wide, wide + size)
    key = turn(key_raw * rms_scale(key_raw) * gains[1:2, :], cosine, sine).astype(bf16)
    value = load_rows(proj, wide + size, wide + 2 * size).astype(bf16)
    for h in range(group):
        low, high = h * size, (h + 1) * size
        query_raw = load_rows(proj, low, high)
        query = turn(query_raw * rms_scale(query_raw) * gains[0:1, :], cosine, sine).astype(bf16)
        prob = softmax_rows(query, key, allowed, scale).astype(bf16)
        mixed = jnp.dot(prob, value, preferred_element_type=f32)
        gate = sigmoid(load_rows(proj, wide + 2 * size + low, wide + 2 * size + high))
        store_rows(gated, low, high, (mixed * gate).astype(bf16))


def backward_kernel(size, group, proj, grad, cos, sin, mask, gains, out, gain_out):
    scale = size ** (-0.5)
    cosine, sine = load_rows(cos, 0, size), load_rows(sin, 0, size)
    allowed = mask[0, 0] > 0.0
    wide = group * size
    gain_q, gain_k = gains[0:1, :], gains[1:2, :]
    key_raw = load_rows(proj, wide, wide + size)
    key_scale = rms_scale(key_raw)
    key = turn(key_raw * key_scale * gain_k, cosine, sine).astype(bf16)
    value = load_rows(proj, wide + size, wide + 2 * size).astype(bf16)
    grad_key = jnp.zeros(key_raw.shape, f32)
    grad_value = jnp.zeros(key_raw.shape, f32)
    sum_q = jnp.zeros((1, size), f32)
    for h in range(group):
        low, high = h * size, (h + 1) * size
        query_raw = load_rows(proj, low, high)
        query_scale = rms_scale(query_raw)
        query = turn(query_raw * query_scale * gain_q, cosine, sine).astype(bf16)
        prob = softmax_rows(query, key, allowed, scale)
        prob_low = prob.astype(bf16)
        mixed = jnp.dot(prob_low, value, preferred_element_type=f32)
        gate = sigmoid(load_rows(proj, wide + 2 * size + low, wide + 2 * size + high))
        incoming = load_rows(grad, low, high)
        grad_mixed = (incoming * gate).astype(bf16)
        grad_gate = (incoming * mixed * gate * (1.0 - gate)).astype(bf16)
        store_rows(out, wide + 2 * size + low, wide + 2 * size + high, grad_gate)
        grad_prob = lax.dot_general(
            grad_mixed, value, (((1,), (1,)), ((), ())), preferred_element_type=f32
        )
        centre = jnp.sum(prob * grad_prob, axis=-1, keepdims=True)
        grad_score = (prob * (grad_prob - centre)).astype(bf16)
        grad_query = jnp.dot(grad_score, key, preferred_element_type=f32) * scale
        grad_key += lax.dot_general(
            grad_score, query, (((0,), (0,)), ((), ())), preferred_element_type=f32
        )
        grad_value += lax.dot_general(
            prob_low, grad_mixed, (((0,), (0,)), ((), ())), preferred_element_type=f32
        )
        raw, addend = norm_back(turn_back(grad_query, cosine, sine), query_raw, query_scale, gain_q)
        sum_q += jnp.sum(addend, axis=0, keepdims=True)
        store_rows(out, low, high, raw.astype(bf16))
    raw, addend = norm_back(turn_back(grad_key * scale, cosine, sine), key_raw, key_scale, gain_k)
    store_rows(out, wide, wide + size, raw.astype(bf16))
    store_rows(out, wide + size, wide + 2 * size, grad_value.astype(bf16))
    gain_out[0, 0, 0:1, :] = sum_q
    gain_out[0, 0, 1:2, :] = jnp.sum(addend, axis=0, keepdims=True)


def rows_spec(rows, width):
    return pl.BlockSpec((1, 2, 1, rows, width), lambda i, m: (i, 0, m, 0, 0))


def attention_forward(proj, tables, gains, group, micro):
    cos, sin, mask = tables
    rows, size = cos.shape[3], cos.shape[4]
    view = proj.reshape(2, 2, micro, rows, proj.shape[1])
    width = (2 * group + 2) * size
    spec = functools.partial(rows_spec, rows)
    out = pl.pallas_call(
        functools.partial(forward_kernel, size, group),
        grid=(2, micro),
        in_specs=[
            spec(width),
            spec(size),
            spec(size),
            pl.BlockSpec((1, 1, 2 * rows, 2 * rows), lambda i, m: (i, m, 0, 0)),
            pl.BlockSpec((2, size), lambda i, m: (0, 0)),
        ],
        out_specs=spec(group * size),
        out_shape=jax.ShapeDtypeStruct((2, 2, micro, rows, group * size), bf16),
        name="attn_fwd",
    )(view, cos, sin, mask, gains)
    return out.reshape(proj.shape[0], group * size)


def attention_backward(proj, grad, tables, gains, group, micro):
    cos, sin, mask = tables
    rows, size = cos.shape[3], cos.shape[4]
    width = (2 * group + 2) * size
    spec = functools.partial(rows_spec, rows)
    out, sums = pl.pallas_call(
        functools.partial(backward_kernel, size, group),
        grid=(2, micro),
        in_specs=[
            spec(width),
            spec(group * size),
            spec(size),
            spec(size),
            pl.BlockSpec((1, 1, 2 * rows, 2 * rows), lambda i, m: (i, m, 0, 0)),
            pl.BlockSpec((2, size), lambda i, m: (0, 0)),
        ],
        out_specs=[
            spec(width),
            pl.BlockSpec((1, 1, 2, size), lambda i, m: (i, m, 0, 0)),
        ],
        out_shape=[
            jax.ShapeDtypeStruct((2, 2, micro, rows, width), bf16),
            jax.ShapeDtypeStruct((2, micro, 2, size), f32),
        ],
        name="attn_bwd",
    )(
        proj.reshape(2, 2, micro, rows, proj.shape[1]),
        grad.reshape(2, 2, micro, rows, grad.shape[1]),
        cos,
        sin,
        mask,
        gains,
    )
    return out.reshape(proj.shape[0], width), jnp.sum(sums, axis=(0, 1))


def make_tables(lengths, side, rows, size):
    inner = jnp.arange(rows, dtype=jnp.int32)
    position = jnp.concatenate([side * rows + inner, (1 - side) * rows + inner])
    ends = jnp.cumsum(lengths, axis=-1, dtype=jnp.int32)
    passed = position[None, None, :, None] >= ends[:, :, None, :]
    doc = jnp.sum(passed.astype(jnp.int32), axis=-1, dtype=jnp.int32)
    starts = jnp.sum(jnp.where(passed, lengths[:, :, None, :], 0), axis=-1, dtype=jnp.int32)
    cos, sin = angle_tables(position - starts, size)
    mask = (doc[:, :, :, None] == doc[:, :, None, :]) & (position[None, :] <= position[:, None])

    def halves(v):
        return v.reshape(2, v.shape[1], 2, rows, size).transpose(0, 2, 1, 3, 4)

    return halves(cos), halves(sin), mask.astype(f32)


def pack_kernel(count, *refs):
    *mats, out = refs
    low = 0
    for mat in mats:
        wide = mat.shape[1] // count
        for i in range(count):
            out[0, i, :, low : low + wide] = mat[:, i * wide : (i + 1) * wide]
        low += wide


def pack_columns(mats, count, copies):
    rows, width = mats[0].shape[0], sum(m.shape[1] for m in mats) // count
    out = pl.pallas_call(
        functools.partial(pack_kernel, count),
        grid=(copies,),
        in_specs=[pl.BlockSpec(m.shape, lambda i: (0, 0)) for m in mats],
        out_specs=pl.BlockSpec((1, count, rows, width), lambda i: (i, 0, 0, 0)),
        out_shape=jax.ShapeDtypeStruct((copies, count, rows, width), mats[0].dtype),
        name="pack_columns",
    )(*mats)
    return out.reshape(copies * count, rows, width)


def unpack_kernel(count, *refs):
    got, *rest = refs
    mats, outs, sums = rest[:count], rest[count:-1], rest[-1]
    copies, pieces = got.shape[:2]
    acc = jnp.zeros(sums.shape, f32)
    for i in range(pieces):
        total = got[0, i].astype(f32)
        for j in range(1, copies):
            total = total + got[j, i].astype(f32)
        low = 0
        for mat, out in zip(mats, outs):
            width = out.shape[1] // pieces
            part, place = total[:, low : low + width], slice(i * width, (i + 1) * width)
            out[:, place] = part
            part = part * mat[:, place].astype(f32)
            for k in range(0, width, 128):
                acc += part[:, k : k + 128]
            low += width
    sums[:, :] = acc


def unpack_columns(got, count, mats):
    copies, rows = got.shape[0] // count, mats[0].shape[0]
    step = min(rows, 32)
    specs = [pl.BlockSpec((step, m.shape[1]), lambda i: (i, 0)) for m in mats]
    *outs, sums = pl.pallas_call(
        functools.partial(unpack_kernel, len(mats)),
        grid=(rows // step,),
        in_specs=[pl.BlockSpec((copies, count, step, got.shape[2]), lambda i: (0, 0, i, 0)), *specs],
        out_specs=[*specs, pl.BlockSpec((step, 128), lambda i: (i, 0))],
        out_shape=[
            *(jax.ShapeDtypeStruct(m.shape, f32) for m in mats),
            jax.ShapeDtypeStruct((rows, 128), f32),
        ],
        name="unpack_columns",
    )(got.reshape(copies, count, *got.shape[1:]), *mats)
    return *outs, jnp.sum(sums, axis=1)


def exchange(blocks, axes):
    return lax.all_to_all(blocks, axes, split_axis=0, concat_axis=0, tiled=True)


def collect(mine, axes, axis):
    return lax.all_gather(mine, axes, axis=axis, tiled=True)


def scatter(full, axes, axis):
    return lax.psum_scatter(full, axes, scatter_dimension=axis, tiled=True)


def route_by(v, pairs):
    return lax.ppermute(v, every, pairs)


every = ("h", "g", "x", "c", "y")


def row_route(ranks, fsdp_count, col_count):
    per = fsdp_count // (ranks * col_count)
    planes = fsdp_count // 4
    pairs = []
    for f in range(fsdp_count):
        for y in range(col_count):
            block, inner = f // per, f % per
            y_to, rest = block // ranks, block % ranks
            plane = inner * col_count + y + rest // 4 * (planes // 2)
            pairs.append((f * col_count + y, (plane * 4 + rest % 4) * col_count + y_to))
    return pairs


def join_rows(full, col_count):
    count, rows, cols = full.shape
    full = full.reshape(count // col_count, col_count, rows, cols).transpose(0, 2, 1, 3)
    return full.reshape(count // col_count * rows, col_count * cols)


def cut_rows(grad, count, col_count):
    rows, cols = grad.shape[0] // (count // col_count), grad.shape[1] // col_count
    blocks = [
        grad[i // col_count * rows :, i % col_count * cols :][:rows, :cols] for i in range(count)
    ]
    return jnp.concatenate(blocks)


def return_rows(blocks, axes, route):
    mine = scatter(blocks, axes, 0)
    return route_by(mine, [(b, a) for a, b in route]).astype(f32)


def inner_body(
    block_input,
    doc_lengths,
    norm_attn,
    w_query,
    w_key,
    w_value,
    w_gate_attn,
    w_out,
    gain_query,
    gain_key,
    norm_ffn,
    w_gate,
    w_up,
    w_down,
    grad_output,
):
    col_count = lax.axis_size("y")
    fsdp_count = 4 * lax.axis_size(data)
    side = lax.axis_index("y")
    micro, _, rows, width = block_input.shape
    size = gain_query.shape[0] * fsdp_count
    group = w_query.shape[1] // w_key.shape[1]
    shards, wide = ("h", "g", "x", "c"), ("h", "x", "c")
    plane_count = fsdp_count // 4
    route_out = row_route(4, fsdp_count, col_count)
    route_down = row_route(8, fsdp_count, col_count)

    tokens_low = block_input.reshape(micro * rows, width)
    cotangent = grad_output.reshape(micro * rows, width)

    flat = doc_lengths.reshape(-1)
    packed = jnp.concatenate([norm_attn, norm_ffn, gain_query, gain_key, flat.astype(bf16)])
    packed = jnp.broadcast_to(packed, (fsdp_count, packed.shape[0]))
    every_gain = exchange(packed, shards).astype(f32)
    every_length = every_gain[:, -flat.shape[0] :].astype(jnp.int32)
    owner = lax.axis_index(shards)
    piece, small = norm_attn.shape[0], gain_query.shape[0]
    gain_one = every_gain[:, :piece].reshape(1, width)
    gain_two = every_gain[:, piece : 2 * piece].reshape(1, width)
    gain_q = every_gain[:, 2 * piece : 2 * piece + small].reshape(1, size)
    gain_k = every_gain[:, 2 * piece + small : 2 * piece + 2 * small].reshape(1, size)
    head_gains = jnp.concatenate([gain_q, gain_k], axis=0)

    def lengths_of(core):
        picked = [every_length[owner ^ core], every_length[owner ^ core ^ 2]]
        return jnp.stack(picked).reshape(2, micro, doc_lengths.shape[2])

    tables = [make_tables(lengths_of(core), side, rows, size) for core in (0, 1)]

    out_moved = route_by(w_out, route_out)
    down_moved = route_by(w_down, route_down)
    packed = pack_columns((w_query, w_key, w_value, w_gate_attn), 4, plane_count)
    packed_wide = pack_columns((w_gate, w_up), 8, 1)
    qkvg = exchange(packed, shards)
    qkvg = qkvg.reshape(width, qkvg.shape[2])
    out_rows = join_rows(collect(out_moved[None], data, 0), col_count)
    down_rows = join_rows(collect(down_moved[None], "g", 0), col_count)
    token_pair = gather_plane(tokens_low, packed_wide)
    spread = exchange(after(packed_wide, qkvg), wide)
    gate_up = collect(spread.reshape(2, -1, spread.shape[2]), "g", 1)
    gate_up = gate_up.reshape(-1, spread.shape[2])
    cot_list = gather_plane(after(cotangent, token_pair[0]))
    far = send_mirror(after(cotangent, qkvg))
    cot_list += gather_plane(after(far, cot_list[0]))

    def first_norm(v):
        v = v.astype(f32)
        return (v * rms_scale(v) * gain_one).astype(bf16)

    def first_part(v, table):
        h = first_norm(v)
        p = dot(h, qkvg, 1, 0)
        return h, p, attention_forward(p, table, head_gains, group, micro)

    other = first_part(token_pair[1], tables[1])
    mine = first_part(after(token_pair[0], other[2]), tables[0])
    hidden, proj, gated = zip(mine, other)
    mixed = fold_cores(dot(gated[0], out_rows, 1, 0), dot(gated[1], out_rows, 1, 0, bf16))
    mixed = finish(*mixed)
    tokens = tokens_low.astype(f32)
    residual = tokens + mixed
    scale_two = rms_scale(residual)
    low = (residual * scale_two * gain_two).astype(bf16)
    far = send_mirror(low)
    hidden_two = gather_plane(low)
    hidden_two += gather_plane(after(far, hidden_two[0]))
    units = gate_up.shape[1] // 2

    inner, grad_units = [], []

    def feed(h, g):
        pre = dot(h, gate_up, 1, 0)
        gate_pre, up_pre = pre[:, :units], pre[:, units:]
        grad_inner = dot(g, down_rows, 1, 1)
        sig = jax.nn.sigmoid(gate_pre)
        act = gate_pre * sig
        zz = (act * up_pre).astype(bf16)
        grad_gate = grad_inner * up_pre * (sig * (1.0 + gate_pre * (1.0 - sig)))
        pair = [grad_gate.astype(bf16), (grad_inner * act).astype(bf16)]
        return zz, jnp.concatenate(pair, axis=1)

    for i in range(4):
        zz, pair = feed(hidden_two[i], cot_list[i])
        inner.append(zz)
        grad_units.append(pair)

    def products(left, right, dim):
        kinds = (f32, bf16, f32, bf16)
        parts = [dot(v, right, 1, dim, kind) for v, kind in zip(left, kinds)]
        return parts[:2], parts[2:]

    def weight_grad(left, right):
        total = dot(left[0], right[0], 0, 0)
        for a, b in zip(left[1:], right[1:]):
            total = total + dot(a, b, 0, 0)
        return total.astype(bf16)

    near_parts, far_parts = products(grad_units, gate_up, 1)
    far_parts, near_parts = fold_cores(*far_parts), fold_cores(*near_parts)
    held = lax.optimization_barrier((*inner, *grad_units, *near_parts[1], *far_parts[1]))
    held_inner, held_units = held[:4], held[4:8]
    sum_down = weight_grad(held_inner, cot_list)
    sum_down = cut_rows(sum_down, plane_count // 2, col_count)
    sum_units = weight_grad(hidden_two, held_units)
    mine = scatter(sum_units.reshape(2, width // 2, 2 * units), "g", 1)
    final_parts = products(held_inner, down_rows, 0)
    held = lax.optimization_barrier((*final_parts[0], *final_parts[1]))
    final_parts = fold_cores(*held[:2]), fold_cores(*held[2:])
    grad_hidden_two = after(finish_pair(near_parts, far_parts), sum_down, sum_units)

    back, _ = norm_back(grad_hidden_two, residual, scale_two, gain_two)
    grad_resid = cotangent.astype(f32) + back
    low_pair = gather_plane(grad_resid.astype(bf16), *final_parts[0][1], *final_parts[1][1])
    got = exchange(mine.reshape(8, mine.shape[1] // 4, mine.shape[2]), wide)
    grad_gate, grad_up, sum_two = unpack_columns(got, 8, (w_gate, w_up))
    grad_down = return_rows(sum_down, "g", route_down)
    sum_out = cut_rows(weight_grad(gated, low_pair), plane_count, col_count)
    grad_out = return_rows(sum_out, data, route_out)
    final = finish_pair(*final_parts)
    block_output = (after(residual, low_pair[0]) + final).astype(bf16).reshape(block_input.shape)
    grad_gated = [dot(low_pair[0], out_rows, 1, 1), dot(after(low_pair[1], sum_out), out_rows, 1, 1)]

    def attention_part(i):
        return attention_backward(proj[i], grad_gated[i], tables[i], head_gains, group, micro)

    backs = [attention_part(0), attention_part(1)]
    grad_proj = [b[0] for b in backs]
    sum_proj = weight_grad(hidden, grad_proj)
    head_sums = (backs[0][1] + backs[1][1]).astype(bf16).reshape(1, 1, 2 * size)
    tail = jnp.pad(head_sums, ((0, 0), (0, 7), (0, sum_proj.shape[1] - 2 * size)))
    tail = jnp.broadcast_to(tail, (fsdp_count, *tail.shape[1:]))
    tail = jnp.concatenate([sum_proj.reshape(fsdp_count, -1, sum_proj.shape[1]), tail], axis=1)
    got = exchange(tail, shards)
    mats = (w_query, w_key, w_value, w_gate_attn)
    grad_query, grad_key, grad_value, grad_gate_attn, sum_one = unpack_columns(got, 4, mats)
    head_sums = jnp.sum(got[:, w_query.shape[0], : 2 * size].astype(f32), axis=0)
    grad_proj = lax.optimization_barrier((*grad_proj, sum_proj, block_output))[:2]
    parts = dot(grad_proj[0], qkvg, 1, 1), dot(grad_proj[1], qkvg, 1, 1, bf16)
    grad_hidden = finish(*fold_cores(*parts))
    back, _ = norm_back(grad_hidden, tokens, rms_scale(tokens), gain_one)
    grad_input = (grad_resid + back).reshape(block_input.shape)

    mine = jnp.concatenate([sum_one, sum_two, head_sums])
    mine = mine + lax.ppermute(mine, "y", swap)
    head_sums = lax.dynamic_slice_in_dim(mine[2 * piece :].reshape(2, size), owner * small, small, 1)
    return (
        block_output,
        grad_input,
        mine[:piece] / norm_attn.astype(f32),
        grad_query,
        grad_key,
        grad_value,
        grad_gate_attn,
        grad_out,
        head_sums[0],
        head_sums[1],
        mine[piece : 2 * piece] / norm_ffn.astype(f32),
        grad_gate,
        grad_up,
        grad_down,
    )


def solution(mesh):
    fsdp_count, col_count = mesh.shape["fsdp"], mesh.shape["col"]
    grid = Mesh(mesh.devices.reshape(2, fsdp_count // 8, 2, 2, col_count), every)
    rows = ("h", "g", "x", "c")
    token, vector, matrix = P(None, rows, "y", None), P(rows), P(rows, "y")
    in_specs = (
        (token, P(None, rows, None), vector)
        + (matrix,) * 5
        + (vector,) * 3
        + (matrix,) * 3
        + (token,)
    )
    out_specs = (token, token, vector) + (matrix,) * 5 + (vector,) * 3 + (matrix,) * 3
    return jax.shard_map(inner_body, mesh=grid, in_specs=in_specs, out_specs=out_specs, check_vma=False)
```
